32 devices in a mesh: dp: 8 (over z, y), mp: 4 (over x, core).
Axes of the slice: x: 2, y: 2, z: 4, core: 2. Of those that a mesh axis runs over, the one named last changes fastest.
Arguments:
- tokens: bfloat16 [1024, 16384], P('dp', 'mp'), may hold values from -6 to 6
- cotangent: bfloat16 [1024, 16384], P('dp', 'mp'), may hold values from -6 to 6
- up_right: bfloat16 [2, 128, 128, 128], P(None, 'mp'), may hold values from -0.5 to 0.5
- up_left: bfloat16 [2, 128, 128, 128], P(None, 'mp'), may hold values from -0.5 to 0.5
- down_first_factor: bfloat16 [2, 128, 128, 128], P(None, 'mp'), may hold values from -0.5 to 0.5
- down_left: bfloat16 [2, 128, 128, 128], P(None, 'mp'), may hold values from -0.5 to 0.5
Outputs:
- mixed: bfloat16 [1024, 16384], P('dp', 'mp')
- tokens_grad: bfloat16 [1024, 16384], P('dp', 'mp')
- grad_up_right: float32 [2, 128, 128, 128], P(None, 'mp', 'dp')
- grad_up_left: float32 [2, 128, 128, 128], P(None, 'mp', 'dp')
- grad_down_right: float32 [2, 128, 128, 128], P(None, 'mp', 'dp')
- grad_down_left: float32 [2, 128, 128, 128], P(None, 'mp', 'dp')
The draws below stay inside these ranges and needn't reach their ends.
All inputs are finite; a program needn't handle non-finite values.
Results may differ from the reference program's by a relative error of at most 0.01.
Values may be sent and summed in bfloat16 or wider, within the bound.
A program may use at most 128 MiB of HBM per device.

```python
import jax
import jax.numpy as jnp
from jax import lax

D = 16384
BLK = 128
NB = 128
Q = 2
TOKENS = 1024
N_DP = 8


def block_scale(key, extent, pieces, smallest, top_value):
    def one(dim, shards_of):
        draws = jax.random.uniform(jax.random.fold_in(jax.random.fold_in(key, 6), dim), (shards_of,), jnp.float32, smallest / len(pieces), top_value / len(pieces))
        return jnp.repeat(jnp.exp(draws), extent[dim] // shards_of).reshape((-1,) + (1,) * (len(extent) - dim - 1))

    gain = one(*pieces[0])
    for cut in pieces[1:]:
        gain = gain * one(*cut)
    return gain


def noise(key, extent, width, bound, shards=(), dtype=jnp.bfloat16):
    result = width * jax.random.normal(key, extent, jnp.float32)
    if shards:
        result = result * block_scale(key, extent, shards, -0.22, 0.18)
    return jnp.clip(result, -bound, bound).astype(dtype)


def setup_inputs(seed: int = 0) -> dict:
    streams_of = jax.random.split(jax.random.key(seed), 7)
    tokens = noise(streams_of[0], (TOKENS, D), 1.0, 6.0, ((0, 8), (1, 4)))
    cotangent = noise(streams_of[1], (TOKENS, D), 1.0, 6.0, ((0, 8), (1, 4)))
    up_right = noise(streams_of[2], (Q, NB, BLK, BLK), BLK ** -0.5, 0.5, ((1, 4),))
    up_left = noise(streams_of[3], (Q, NB, NB, BLK), NB ** -0.5, 0.5, ((1, 4),))
    down_first_factor = noise(streams_of[4], (Q, NB, BLK, BLK), BLK ** -0.5, 0.5, ((1, 4),))
    down_left = noise(streams_of[5], (Q, NB, NB, BLK), NB ** -0.5, 0.5, ((1, 4),))
    return dict(tokens=tokens, cotangent=cotangent, up_right=up_right, up_left=up_left, down_first_factor=down_first_factor, down_left=down_left)


gelu_root = 0.7978845608
gelu_cube = 0.044715


def gelu_value(pre_values):
    inner_arg = gelu_root * (pre_values + gelu_cube * pre_values * pre_values * pre_values)
    return 0.5 * pre_values * (1.0 + jnp.tanh(inner_arg))


def gelu_slope(pre_values):
    inner_arg = gelu_root * (pre_values + gelu_cube * pre_values * pre_values * pre_values)
    tanh_term = jnp.tanh(inner_arg)
    return 0.5 * (1.0 + tanh_term) + 0.5 * pre_values * (1.0 - tanh_term * tanh_term) * gelu_root * (1.0 + 3.0 * gelu_cube * pre_values * pre_values)


def shard_partials(einsum_form, first_arr, second_arr):
    first_split = first_arr.reshape((N_DP, TOKENS // N_DP) + first_arr.shape[1:])
    second_split = second_arr.reshape((N_DP, TOKENS // N_DP) + second_arr.shape[1:])
    partial_terms = jnp.einsum(einsum_form, first_split, second_split)
    rounded = lax.optimization_barrier(partial_terms.astype(jnp.bfloat16))
    return jnp.sum(rounded.astype(jnp.float32), axis=0) * (TOKENS ** -0.5)


def reference(tokens, cotangent, up_right, up_left, down_first_factor, down_left):
    blocked_in = tokens.reshape(TOKENS, NB, BLK).astype(jnp.float32)
    upstream = cotangent.reshape(TOKENS, NB, BLK).astype(jnp.float32)
    out_acc = jnp.zeros((TOKENS, NB, BLK), jnp.float32)
    grad_acc = jnp.zeros((TOKENS, NB, BLK), jnp.float32)
    list_ur, list_ul, list_dr, list_dl = [], [], [], []
    for fourth_part in range(Q):
        weight_ur = up_right[fourth_part].astype(jnp.float32)
        up_left_weight = up_left[fourth_part].astype(jnp.float32)
        weight_dr = down_first_factor[fourth_part].astype(jnp.float32)
        weight_dl = down_left[fourth_part].astype(jnp.float32)
        right_factor_output = jnp.einsum("tij,ijc->tic", blocked_in, weight_ur).astype(jnp.bfloat16).astype(jnp.float32)
        preactivation_values = jnp.einsum("fuh,hul->fhl", right_factor_output, up_left_weight)
        hidden = gelu_value(preactivation_values).astype(jnp.bfloat16).astype(jnp.float32)
        down_panel = jnp.einsum("tca,cae->tce", hidden, weight_dr).astype(jnp.bfloat16).astype(jnp.float32)
        out_acc = out_acc + jnp.einsum("tce,ecf->tef", down_panel, weight_dl)
        list_dl.append(shard_partials("stce,stef->secf", down_panel, upstream))
        down_grad = jnp.einsum("tef,ecf->tce", upstream, weight_dl).astype(jnp.bfloat16).astype(jnp.float32)
        hidden_grad = jnp.einsum("tce,cae->tca", down_grad, weight_dr)
        list_dr.append(shard_partials("stca,stce->scae", hidden, down_grad))
        preactivation_gradient = (hidden_grad * gelu_slope(preactivation_values)).astype(jnp.bfloat16).astype(jnp.float32)
        list_ul.append(shard_partials("stac,stcb->scab", right_factor_output, preactivation_gradient))
        right_factor_gradient = jnp.einsum("gdw,dsw->gsd", preactivation_gradient, up_left_weight).astype(jnp.bfloat16).astype(jnp.float32)
        list_ur.append(shard_partials("stij,stic->sijc", blocked_in, right_factor_gradient))
        grad_acc = grad_acc + jnp.einsum("tic,ijc->tij", right_factor_gradient, weight_ur)
    mixed = out_acc.reshape(TOKENS, D).astype(jnp.bfloat16)
    tokens_grad = grad_acc.reshape(TOKENS, D).astype(jnp.bfloat16)
    return (mixed, tokens_grad, jnp.stack(list_ur), jnp.stack(list_ul), jnp.stack(list_dr), jnp.stack(list_dl))
```

```python
import jax
import jax.numpy as jnp
from jax import lax
from jax.sharding import PartitionSpec as P

gelu_root = 0.7978845608
gelu_cube = 0.044715


def gelu_value(pre_values):
    inner_arg = gelu_root * (pre_values + gelu_cube * pre_values * pre_values * pre_values)
    return 0.5 * pre_values * (1.0 + jnp.tanh(inner_arg))


def gelu_slope(pre_values):
    inner_arg = gelu_root * (pre_values + gelu_cube * pre_values * pre_values * pre_values)
    tanh_term = jnp.tanh(inner_arg)
    return 0.5 * (1.0 + tanh_term) + 0.5 * pre_values * (
        1.0 - tanh_term * tanh_term
    ) * gelu_root * (1.0 + 3.0 * gelu_cube * pre_values * pre_values)


def partner_cross(panel_data, split_dim, concat_dim):
    return lax.all_to_all(panel_data, "mp", split_dim, concat_dim, tiled=True)


def forward_cross(panel_data, work_fn):
    return work_fn(partner_cross(panel_data, 2, 1))


def backward_cross(panel_data, work_fn):
    return work_fn(partner_cross(panel_data, 1, 2))


def body(tokens, cotangent, up_right, up_left, down_first_factor, down_left):
    tok_rows = tokens.shape[0]
    blocks_here = up_right.shape[1]
    block_width = up_right.shape[2]
    inputs = tokens.reshape(tok_rows, blocks_here, block_width)
    upstream = cotangent.reshape(tok_rows, blocks_here, block_width)
    right_panel = jnp.einsum(
        "tij,qijc->qict", inputs, up_right, preferred_element_type=jnp.float32
    ).astype(jnp.bfloat16)

    def up_work(crossed):
        return (
            crossed,
            jnp.einsum("qact,qcab->qcbt", crossed, up_left, preferred_element_type=jnp.float32),
        )

    crossed_up, preactivation_values = forward_cross(right_panel, up_work)
    hidden = gelu_value(preactivation_values).astype(jnp.bfloat16)
    down_panel = jnp.einsum(
        "qcat,qcae->qcet", hidden, down_first_factor, preferred_element_type=jnp.float32
    ).astype(jnp.bfloat16)

    def down_work(crossed):
        return (
            crossed,
            jnp.einsum("qcet,qecf->eft", crossed, down_left, preferred_element_type=jnp.float32)[
                None
            ],
        )

    crossed_down, summed = forward_cross(down_panel, down_work)
    mixed = jnp.transpose(summed[0], (2, 0, 1)).reshape(tok_rows, -1).astype(jnp.bfloat16)
    grad_down_left = jnp.einsum(
        "qcet,tef->qecf", crossed_down, upstream, preferred_element_type=jnp.float32
    )
    back_panel = jnp.einsum(
        "tef,qecf->qcet", upstream, down_left, preferred_element_type=jnp.float32
    ).astype(jnp.bfloat16)

    def down_back(crossed):
        return (
            crossed,
            jnp.einsum(
                "qcet,qcae->qcat", crossed, down_first_factor, preferred_element_type=jnp.float32
            ),
        )

    down_grad, hidden_grad = backward_cross(back_panel, down_back)
    grad_down_right = jnp.einsum(
        "qcat,qcet->qcae", hidden, down_grad, preferred_element_type=jnp.float32
    )
    grad_scale = (lax.axis_size("dp") * tok_rows) ** (-0.5)
    preactivation_gradient = (hidden_grad * gelu_slope(preactivation_values)).astype(jnp.bfloat16)
    grad_up_left = jnp.einsum(
        "qact,qcbt->qcab", crossed_up, preactivation_gradient, preferred_element_type=jnp.float32
    )
    up_back_panel = jnp.einsum(
        "qcbt,qcab->qact", preactivation_gradient, up_left, preferred_element_type=jnp.float32
    ).astype(jnp.bfloat16)

    def up_back(crossed):
        return (
            crossed,
            jnp.einsum("qict,qijc->ijt", crossed, up_right, preferred_element_type=jnp.float32)[
                None
            ],
        )

    right_factor_gradient, input_grad = backward_cross(up_back_panel, up_back)
    grad_up_right = jnp.einsum(
        "tij,qict->qijc", inputs, right_factor_gradient, preferred_element_type=jnp.float32
    )
    tokens_grad = jnp.transpose(input_grad[0], (2, 0, 1)).reshape(tok_rows, -1).astype(jnp.bfloat16)
    reduced = (
        lax.psum_scatter(
            grad_up_right.astype(jnp.bfloat16), "dp", scatter_dimension=2, tiled=True
        ).astype(jnp.float32),
        lax.psum_scatter(
            grad_up_left.astype(jnp.bfloat16), "dp", scatter_dimension=2, tiled=True
        ).astype(jnp.float32),
        lax.psum_scatter(
            grad_down_right.astype(jnp.bfloat16), "dp", scatter_dimension=2, tiled=True
        ).astype(jnp.float32),
        lax.psum_scatter(
            grad_down_left.astype(jnp.bfloat16), "dp", scatter_dimension=2, tiled=True
        ).astype(jnp.float32),
    )
    return (
        mixed,
        tokens_grad,
        reduced[0] * grad_scale,
        reduced[1] * grad_scale,
        reduced[2] * grad_scale,
        reduced[3] * grad_scale,
    )


def solution(mesh):
    in_specs = (
        P("dp", "mp"),
        P("dp", "mp"),
        P(None, "mp", None, None),
        P(None, "mp", None, None),
        P(None, "mp", None, None),
        P(None, "mp", None, None),
    )
    out_specs = (
        P("dp", "mp"),
        P("dp", "mp"),
        P(None, "mp", "dp", None),
        P(None, "mp", "dp", None),
        P(None, "mp", "dp", None),
        P(None, "mp", "dp", None),
    )
    return jax.shard_map(body, mesh=mesh, in_specs=in_specs, out_specs=out_specs, check_vma=False)
```

```python
import functools

import jax
import jax.numpy as jnp
from jax import lax
from jax.experimental import pallas as pl
from jax.experimental.pallas import tpu as pltpu
from jax.sharding import PartitionSpec as P

gelu_root = 0.7978845608
gelu_cube = 0.044715
F32 = jnp.float32
BF16 = jnp.bfloat16


def mm(lhs, rhs, ldim, rdim):
    return lax.dot_general(lhs, rhs, (((ldim,), (rdim,)), ((), ())), preferred_element_type=F32)


def send_panel(outs, scratch, me, blocks):
    span = blocks * blocks
    for k, out in enumerate(outs):
        start = pl.multiple_of((me ^ k) * span, span)
        rows = scratch[pl.ds(start, span), :]
        out[...] = rows.reshape(out.shape).astype(BF16)


def gather_rows(parts, scratch, me, block, blocks):
    for k, part in enumerate(parts):
        start = pl.multiple_of((me ^ k) * blocks, blocks)
        scratch[pl.ds(start, blocks), :] = part[block].astype(F32)
    return scratch[...].astype(BF16)


def store_grad(keep, send, kind, block, value, scratch, me, ways):
    rows = value.shape[0] // ways
    scratch[...] = value
    for p in range(ways // 2):
        k = 2 * p
        for out, rel in ((keep, k), (send, k + 1)):
            start = pl.multiple_of((me ^ rel) * rows, rows)
            out[p, kind, block] = scratch[pl.ds(start, rows), :].astype(BF16)


def panel_kernel(ways, wdim, me_ref, x_ref, w_ref, *rest):
    outs, scratch = rest[:ways], rest[ways]
    blocks, width = w_ref.shape[1], w_ref.shape[2]
    me = me_ref[0]
    for i in range(blocks):
        value = mm(w_ref[0, i], x_ref[:, i * width : (i + 1) * width], wdim, 1)
        scratch[pl.ds(i, width, stride=blocks), :] = value
    send_panel(outs, scratch, me, blocks)


def make_panel(me, x, w, q, ways, wdim):
    tok, width = x.shape[0], w.shape[-1]
    blocks = w.shape[1]
    part = jax.ShapeDtypeStruct((blocks, blocks, tok), BF16)
    return pl.pallas_call(
        functools.partial(panel_kernel, ways, wdim),
        out_shape=[part] * ways,
        grid=(1,),
        in_specs=[
            pl.BlockSpec(memory_space=pltpu.SMEM),
            pl.BlockSpec(x.shape, lambda s: (0, 0)),
            pl.BlockSpec((1,) + w.shape[1:], lambda s: (q, 0, 0, 0)),
        ],
        out_specs=[pl.BlockSpec(part.shape, lambda s: (0, 0, 0))] * ways,
        scratch_shapes=[pltpu.VMEM((width * blocks, tok), F32)],
        compiler_params=pltpu.CompilerParams(vmem_limit_bytes=40 * 2**20),
        cost_estimate=pl.CostEstimate(flops=2 * tok * x.shape[1] * width * 8, bytes_accessed=4 * 2**20, transcendentals=0),
    )(me, x, w)


def middle_kernel(mp_ways, dp_ways, me_ref, ul_ref, df_ref, *rest):
    n = mp_ways
    r_in, b_in = rest[:n], rest[n : 2 * n]
    d_out, u_out = rest[2 * n : 3 * n], rest[3 * n : 4 * n]
    keep, send = rest[4 * n], rest[4 * n + 1]
    scr_d, scr_u, asm_r, asm_b, gr1, gr2 = rest[4 * n + 2 :]
    blocks, width = ul_ref.shape[1], ul_ref.shape[2]
    me_mp, me_dp = me_ref[0], me_ref[1]

    def step(c, carry):
        ul, df = ul_ref[0, c], df_ref[0, c]
        cu = gather_rows(r_in, asm_r, me_mp, c, blocks)
        dg = gather_rows(b_in, asm_b, me_mp, c, blocks)
        pre = mm(ul, cu, 0, 0)
        sq = pre * pre
        th = jnp.tanh(gelu_root * (pre + gelu_cube * sq * pre))
        half = 0.5 * (1.0 + th)
        hidden = (pre * half).astype(BF16)
        slope = half + 0.5 * pre * (1.0 - th * th) * (gelu_root * (1.0 + 3.0 * gelu_cube * sq))
        scr_d[pl.ds(c, width, stride=blocks), :] = mm(df, hidden, 0, 0)
        pg = (mm(df, dg, 1, 0) * slope).astype(BF16)
        scr_u[pl.ds(c, width, stride=blocks), :] = mm(ul, pg, 1, 0)
        store_grad(keep, send, 0, c, mm(hidden, dg, 1, 1), gr1, me_dp, dp_ways)
        store_grad(keep, send, 1, c, mm(cu, pg, 1, 1), gr2, me_dp, dp_ways)
        return carry

    lax.fori_loop(0, blocks, step, 0)
    send_panel(d_out, scr_d, me_mp, blocks)
    send_panel(u_out, scr_u, me_mp, blocks)


def grad_halves(blocks, width, dp_ways):
    return jax.ShapeDtypeStruct((dp_ways // 2, 2, blocks, width // dp_ways, width), BF16)


def full_spec(shape):
    return pl.BlockSpec(shape, lambda s: (0,) * len(shape))


def make_middle(me, r_in, b_in, ul, df, q, dp_ways):
    n = len(r_in)
    part = jax.ShapeDtypeStruct(r_in[0].shape, BF16)
    blocks, width, tok = ul.shape[1], ul.shape[2], part.shape[2]
    half = grad_halves(blocks, width, dp_ways)
    w_spec = pl.BlockSpec((1,) + ul.shape[1:], lambda s: (q, 0, 0, 0))
    res = pl.pallas_call(
        functools.partial(middle_kernel, n, dp_ways),
        out_shape=[part] * (2 * n) + [half] * 2,
        grid=(1,),
        in_specs=[pl.BlockSpec(memory_space=pltpu.SMEM), w_spec, w_spec] + [full_spec(part.shape)] * (2 * n),
        out_specs=[full_spec(part.shape)] * (2 * n) + [full_spec(half.shape)] * 2,
        scratch_shapes=[pltpu.VMEM((width * blocks, tok), F32)] * 2
        + [pltpu.VMEM((width, tok), F32)] * 2
        + [pltpu.VMEM((width, width), F32)] * 2,
        compiler_params=pltpu.CompilerParams(vmem_limit_bytes=40 * 2**20),
        cost_estimate=pl.CostEstimate(flops=6 * 2 * tok * blocks * width * width * 8, bytes_accessed=8 * 2**20, transcendentals=0),
    )(me, ul, df, *r_in, *b_in)
    return res[:n], res[n : 2 * n], res[2 * n], res[2 * n + 1]


def last_grads_kernel(mp_ways, dp_ways, me_ref, x_ref, g_ref, *rest):
    n = mp_ways
    d_in, u_in = rest[:n], rest[n : 2 * n]
    keep, send, asm_d, asm_u, gr1, gr2 = rest[2 * n :]
    blocks = d_in[0].shape[0]
    width = gr1.shape[0]
    me_mp, me_dp = me_ref[0], me_ref[1]

    for e in range(blocks):
        cols = slice(e * width, (e + 1) * width)
        cd = gather_rows(d_in, asm_d, me_mp, e, blocks)
        rg = gather_rows(u_in, asm_u, me_mp, e, blocks)
        store_grad(keep, send, 0, e, mm(cd, g_ref[:, cols], 1, 0), gr1, me_dp, dp_ways)
        store_grad(keep, send, 1, e, mm(rg, x_ref[:, cols], 1, 0).T, gr2, me_dp, dp_ways)


def make_last_grads(me, d_in, u_in, x, g, width, dp_ways):
    n = len(d_in)
    part = d_in[0]
    blocks, tok = part.shape[0], part.shape[2]
    half = grad_halves(blocks, width, dp_ways)
    return pl.pallas_call(
        functools.partial(last_grads_kernel, n, dp_ways),
        out_shape=[half] * 2,
        grid=(1,),
        in_specs=[pl.BlockSpec(memory_space=pltpu.SMEM)] + [full_spec(x.shape)] * 2 + [full_spec(part.shape)] * (2 * n),
        out_specs=[full_spec(half.shape)] * 2,
        scratch_shapes=[pltpu.VMEM((width, tok), F32)] * 2 + [pltpu.VMEM((width, width), F32)] * 2,
        compiler_params=pltpu.CompilerParams(vmem_limit_bytes=40 * 2**20),
        cost_estimate=pl.CostEstimate(flops=2 * 2 * tok * blocks * width * width * 8, bytes_accessed=6 * 2**20, transcendentals=0),
    )(me, x, g, *d_in, *u_in)


def outputs_kernel(mp_ways, me_ref, dl_ref, ur_ref, *rest):
    n = mp_ways
    groups = dl_ref.shape[0]
    count = groups * n
    d_in, u_in = rest[:count], rest[count : 2 * count]
    mixed, tgrad, asm_d, asm_u = rest[2 * count :]
    blocks, width = dl_ref.shape[1], dl_ref.shape[2]
    me_mp = me_ref[0]
    for e in range(blocks):
        cols = slice(e * width, (e + 1) * width)
        out_sum = grad_sum = None
        for q in range(groups):
            cd = gather_rows(d_in[q * n : (q + 1) * n], asm_d, me_mp, e, blocks)
            rg = gather_rows(u_in[q * n : (q + 1) * n], asm_u, me_mp, e, blocks)
            one = mm(cd, dl_ref[q, e], 0, 0)
            two = mm(ur_ref[q, e], rg, 1, 0)
            out_sum = one if q == 0 else out_sum + one
            grad_sum = two if q == 0 else grad_sum + two
        mixed[:, cols] = out_sum.astype(BF16)
        tgrad[:, cols] = grad_sum.T.astype(BF16)


def make_outputs(me, d_in, u_in, dl, ur):
    n = len(d_in[0])
    part = d_in[0][0]
    groups, blocks, width, tok = dl.shape[0], dl.shape[1], dl.shape[2], part.shape[2]
    flat_d = [p for d in d_in for p in d]
    flat_u = [p for u in u_in for p in u]
    out = jax.ShapeDtypeStruct((tok, blocks * width), BF16)
    return pl.pallas_call(
        functools.partial(outputs_kernel, n),
        out_shape=[out] * 2,
        grid=(1,),
        in_specs=[pl.BlockSpec(memory_space=pltpu.SMEM)]
        + [full_spec(dl.shape)] * 2
        + [full_spec(part.shape)] * (2 * n * groups),
        out_specs=[full_spec(out.shape)] * 2,
        scratch_shapes=[pltpu.VMEM((width, tok), F32)] * 2,
        compiler_params=pltpu.CompilerParams(vmem_limit_bytes=40 * 2**20),
        cost_estimate=pl.CostEstimate(flops=4 * 2 * tok * blocks * width * width * 8, bytes_accessed=10 * 2**20, transcendentals=0),
    )(me, dl, ur, *flat_d, *flat_u)


def xor_permute(array, axis, k):
    return lax.ppermute(array, axis, [(i, i ^ k) for i in range(lax.axis_size(axis))])


def exchange(parts):
    return [p if k == 0 else xor_permute(p, "mp", k) for k, p in enumerate(parts)]


def halving_sum(keep, send, scale):
    bit = 1
    while True:
        got = xor_permute(send, "dp", bit)
        total = keep.astype(F32) + got.astype(F32)
        if total.shape[0] == 1:
            return total[0] * scale
        total = total.astype(BF16).reshape((total.shape[0] // 2, 2) + total.shape[1:])
        keep, send = total[:, 0], total[:, 1]
        bit *= 2


def body(tokens, cotangent, up_right, up_left, down_first_factor, down_left):
    groups, width = up_right.shape[0], up_right.shape[2]
    mp_ways, dp_ways = lax.axis_size("mp"), lax.axis_size("dp")
    scale = (dp_ways * tokens.shape[0]) ** (-0.5)
    me = jnp.stack([lax.axis_index("mp"), lax.axis_index("dp")]).astype(jnp.int32)
    rights, backs = [], []
    for q in range(groups):
        rights.append(exchange(make_panel(me, tokens, up_right, q, mp_ways, 0)))
        backs.append(exchange(make_panel(me, cotangent, down_left, q, mp_ways, 1)))
    downs, ups, mid_sums, last_sums = [], [], [], []
    for q in range(groups):
        d, u, keep, send = make_middle(me, rights[q], backs[q], up_left, down_first_factor, q, dp_ways)
        downs.append(exchange(d))
        ups.append(exchange(u))
        mid_sums.append(halving_sum(keep, send, scale))
    for q in range(groups):
        keep, send = make_last_grads(me, downs[q], ups[q], tokens, cotangent, width, dp_ways)
        last_sums.append(halving_sum(keep, send, scale))
    mixed, tokens_grad = make_outputs(me, downs, ups, down_left, up_right)

    def pick(sums, kind):
        return jnp.stack([s[kind] for s in sums])

    return (mixed, tokens_grad, pick(last_sums, 1), pick(mid_sums, 1), pick(mid_sums, 0), pick(last_sums, 0))


def solution(mesh):
    weight = P(None, "mp", None, None)
    in_specs = (P("dp", "mp"), P("dp", "mp"), weight, weight, weight, weight)
    grad = P(None, "mp", "dp", None)
    out_specs = (P("dp", "mp"), P("dp", "mp"), grad, grad, grad, grad)
    return jax.shard_map(body, mesh=mesh, in_specs=in_specs, out_specs=out_specs, check_vma=False)
```

```python
import functools

import jax
import jax.numpy as jnp
from jax import lax
from jax.experimental import pallas as pl
from jax.experimental.pallas import tpu as pltpu
from jax.sharding import PartitionSpec as P

gelu_root = 0.7978845608
gelu_cube = 0.044715
F32 = jnp.float32
BF16 = jnp.bfloat16


def mm(lhs, rhs, ldim, rdim):
    return lax.dot_general(lhs, rhs, (((ldim,), (rdim,)), ((), ())), preferred_element_type=F32)


def send_panel(outs, kind, scratch, me, blocks):
    span = blocks * blocks
    for k, out in enumerate(outs):
        start = pl.multiple_of((me ^ k) * span, span)
        rows = scratch[pl.ds(start, span), :]
        out[kind] = rows.reshape(out.shape[1:]).astype(BF16)


def gather_rows(parts, kind, scratch, slot, me, block, blocks):
    for k, part in enumerate(parts):
        start = pl.multiple_of((me ^ k) * blocks, blocks)
        scratch[slot, pl.ds(start, blocks), :] = part[kind, block].astype(F32)
    return scratch[slot].astype(BF16)


def hop_order(ways, kind):
    bits = [1 << b for b in range(ways.bit_length() - 1)]
    return [bits[1], bits[0]] + bits[2:] if kind and len(bits) > 1 else bits


def store_grad(outs, kind, block, value, scratch, slot, me, ways):
    rows = value.shape[0] // ways
    first, *later = hop_order(ways, kind)
    scratch[slot] = value
    for p in range(ways // 2):
        rel = sum(bit for t, bit in enumerate(later) if p >> t & 1)
        for out, target in ((outs[2 * kind], rel), (outs[2 * kind + 1], rel + first)):
            start = pl.multiple_of((me ^ target) * rows, rows)
            out[p, block] = scratch[slot, pl.ds(start, rows), :].astype(BF16)


def panels_kernel(ways, me_ref, x_ref, g_ref, ur_ref, dl_ref, *rest):
    outs, scr_r, scr_b = rest[:ways], rest[ways], rest[ways + 1]
    blocks, width = ur_ref.shape[1], ur_ref.shape[2]
    me = me_ref[0]
    for i in range(blocks):
        cols = slice(i * width, (i + 1) * width)
        scr_r[pl.ds(i, width, stride=blocks), :] = mm(ur_ref[0, i], x_ref[:, cols], 0, 1)
        scr_b[pl.ds(i, width, stride=blocks), :] = mm(dl_ref[0, i], g_ref[:, cols], 1, 1)
    send_panel(outs, 0, scr_r, me, blocks)
    send_panel(outs, 1, scr_b, me, blocks)


def full_spec(shape):
    return pl.BlockSpec(shape, lambda s: (0,) * len(shape))


def group_spec(w, q):
    return pl.BlockSpec((1,) + w.shape[1:], lambda s: (q, 0, 0, 0))


def limits(flops, mib):
    return dict(
        compiler_params=pltpu.CompilerParams(vmem_limit_bytes=40 * 2**20),
        cost_estimate=pl.CostEstimate(flops=flops * 8, bytes_accessed=mib * 2**20, transcendentals=0),
    )


def make_panels(me, x, g, ur, dl, q, ways):
    tok, blocks, width = x.shape[0], ur.shape[1], ur.shape[2]
    part = jax.ShapeDtypeStruct((2, blocks, blocks, tok), BF16)
    return pl.pallas_call(
        functools.partial(panels_kernel, ways),
        out_shape=[part] * ways,
        grid=(1,),
        in_specs=[
            pl.BlockSpec(memory_space=pltpu.SMEM),
            full_spec(x.shape),
            full_spec(g.shape),
            group_spec(ur, q),
            group_spec(dl, q),
        ],
        out_specs=[full_spec(part.shape)] * ways,
        scratch_shapes=[pltpu.VMEM((width * blocks, tok), F32)] * 2,
        **limits(4 * tok * blocks * width * width, 8),
    )(me, x, g, ur, dl)


UNROLL = 4


def middle_kernel(mp_ways, dp_ways, me_ref, ul_ref, df_ref, *rest):
    n = mp_ways
    first_in, outs, grads = rest[:n], rest[n : 2 * n], rest[2 * n : 2 * n + 4]
    scr_d, scr_u, asm_r, asm_b, gr1, gr2 = rest[2 * n + 4 :]
    blocks, width = ul_ref.shape[1], ul_ref.shape[2]
    me_mp, me_dp = me_ref[0], me_ref[1]

    def one(c, slot):
        ul, df = ul_ref[0, c], df_ref[0, c]
        cu = gather_rows(first_in, 0, asm_r, slot, me_mp, c, blocks)
        dg = gather_rows(first_in, 1, asm_b, slot, me_mp, c, blocks)
        pre = mm(ul, cu, 0, 0)
        sq = pre * pre
        th = jnp.tanh(gelu_root * (pre + gelu_cube * sq * pre))
        half = 0.5 * (1.0 + th)
        hidden = (pre * half).astype(BF16)
        slope = half + 0.5 * pre * (1.0 - th * th) * (gelu_root * (1.0 + 3.0 * gelu_cube * sq))
        scr_d[pl.ds(c, width, stride=blocks), :] = mm(df, hidden, 0, 0)
        pg = (mm(df, dg, 1, 0) * slope).astype(BF16)
        scr_u[pl.ds(c, width, stride=blocks), :] = mm(ul, pg, 1, 0)
        store_grad(grads, 0, c, mm(hidden, dg, 1, 1), gr1, slot, me_dp, dp_ways)
        store_grad(grads, 1, c, mm(cu, pg, 1, 1), gr2, slot, me_dp, dp_ways)

    def step(s, carry):
        for slot in range(UNROLL):
            one(s * UNROLL + slot, slot)
        return carry

    lax.fori_loop(0, blocks // UNROLL, step, 0)
    send_panel(outs, 0, scr_d, me_mp, blocks)
    send_panel(outs, 1, scr_u, me_mp, blocks)


def grad_halves(blocks, width, dp_ways):
    return jax.ShapeDtypeStruct((dp_ways // 2, blocks, width // dp_ways, width), BF16)


def make_middle(me, first_in, ul, df, q, dp_ways):
    n = len(first_in)
    part = jax.ShapeDtypeStruct(first_in[0].shape, BF16)
    blocks, width, tok = ul.shape[1], ul.shape[2], part.shape[3]
    half = grad_halves(blocks, width, dp_ways)
    res = pl.pallas_call(
        functools.partial(middle_kernel, n, dp_ways),
        out_shape=[part] * n + [half] * 4,
        grid=(1,),
        in_specs=[pl.BlockSpec(memory_space=pltpu.SMEM)] + [group_spec(ul, q)] * 2 + [full_spec(part.shape)] * n,
        out_specs=[full_spec(part.shape)] * n + [full_spec(half.shape)] * 4,
        scratch_shapes=[pltpu.VMEM((width * blocks, tok), F32)] * 2
        + [pltpu.VMEM((UNROLL, width, tok), F32)] * 2
        + [pltpu.VMEM((UNROLL, width, width), F32)] * 2,
        **limits(12 * tok * blocks * width * width, 8),
    )(me, ul, df, *first_in)
    return res[:n], res[n:]


def last_grads_kernel(mp_ways, dp_ways, me_ref, x_ref, g_ref, *rest):
    n = mp_ways
    second_in, grads = rest[:n], rest[n : n + 4]
    asm_d, asm_u, gr1, gr2 = rest[n + 4 :]
    blocks = second_in[0].shape[1]
    width = gr1.shape[1]
    me_mp, me_dp = me_ref[0], me_ref[1]
    for e in range(blocks):
        cols = slice(e * width, (e + 1) * width)
        slot = e % UNROLL
        cd = gather_rows(second_in, 0, asm_d, slot, me_mp, e, blocks)
        rg = gather_rows(second_in, 1, asm_u, slot, me_mp, e, blocks)
        store_grad(grads, 0, e, mm(cd, g_ref[:, cols], 1, 0), gr1, slot, me_dp, dp_ways)
        store_grad(grads, 1, e, mm(rg, x_ref[:, cols], 1, 0).T, gr2, slot, me_dp, dp_ways)


def make_last_grads(me, second_in, x, g, width, dp_ways):
    n = len(second_in)
    part = second_in[0]
    blocks, tok = part.shape[1], part.shape[3]
    half = grad_halves(blocks, width, dp_ways)
    return pl.pallas_call(
        functools.partial(last_grads_kernel, n, dp_ways),
        out_shape=[half] * 4,
        grid=(1,),
        in_specs=[pl.BlockSpec(memory_space=pltpu.SMEM)] + [full_spec(x.shape)] * 2 + [full_spec(part.shape)] * n,
        out_specs=[full_spec(half.shape)] * 4,
        scratch_shapes=[pltpu.VMEM((UNROLL, width, tok), F32)] * 2 + [pltpu.VMEM((UNROLL, width, width), F32)] * 2,
        **limits(4 * tok * blocks * width * width, 6),
    )(me, x, g, *second_in)


def outputs_kernel(mp_ways, me_ref, dl_ref, ur_ref, *rest):
    n = mp_ways
    groups = dl_ref.shape[0]
    second_in = rest[: groups * n]
    mixed, tgrad, asm_d, asm_u = rest[groups * n :]
    blocks, width = dl_ref.shape[1], dl_ref.shape[2]
    me_mp = me_ref[0]
    for e in range(blocks):
        cols = slice(e * width, (e + 1) * width)
        out_sum = grad_sum = None
        for q in range(groups):
            parts = second_in[q * n : (q + 1) * n]
            slot = (e * groups + q) % UNROLL
            cd = gather_rows(parts, 0, asm_d, slot, me_mp, e, blocks)
            rg = gather_rows(parts, 1, asm_u, slot, me_mp, e, blocks)
            one = mm(cd, dl_ref[q, e], 0, 0)
            two = mm(ur_ref[q, e], rg, 1, 0)
            out_sum = one if q == 0 else out_sum + one
            grad_sum = two if q == 0 else grad_sum + two
        mixed[:, cols] = out_sum.astype(BF16)
        tgrad[:, cols] = grad_sum.T.astype(BF16)


def make_outputs(me, second_in, dl, ur):
    n = len(second_in[0])
    part = second_in[0][0]
    groups, blocks, width, tok = dl.shape[0], dl.shape[1], dl.shape[2], part.shape[3]
    out = jax.ShapeDtypeStruct((tok, blocks * width), BF16)
    return pl.pallas_call(
        functools.partial(outputs_kernel, n),
        out_shape=[out] * 2,
        grid=(1,),
        in_specs=[pl.BlockSpec(memory_space=pltpu.SMEM)]
        + [full_spec(dl.shape)] * 2
        + [full_spec(part.shape)] * (n * groups),
        out_specs=[full_spec(out.shape)] * 2,
        scratch_shapes=[pltpu.VMEM((UNROLL, width, tok), F32)] * 2,
        **limits(8 * tok * blocks * width * width, 10),
    )(me, dl, ur, *[p for parts in second_in for p in parts])


def xor_permute(array, axis, k):
    return lax.ppermute(array, axis, [(i, i ^ k) for i in range(lax.axis_size(axis))])


def exchange(parts):
    return [p if k == 0 else xor_permute(p, "mp", k) for k, p in enumerate(parts)]


def halving_sums(halves, scale):
    ways = lax.axis_size("dp")
    pairs = [[halves[0], halves[1]], [halves[2], halves[3]]]
    orders = [hop_order(ways, kind) for kind in range(2)]
    sums = [None, None]
    for hop in range(len(orders[0])):
        for kind in range(2):
            keep, send = pairs[kind]
            got = xor_permute(send, "dp", orders[kind][hop])
            total = keep.astype(F32) + got.astype(F32)
            if total.shape[0] == 1:
                sums[kind] = total[0] * scale
                continue
            total = total.astype(BF16).reshape((total.shape[0] // 2, 2) + total.shape[1:])
            pairs[kind] = [total[:, 0], total[:, 1]]
    return sums


def body(tokens, cotangent, up_right, up_left, down_first_factor, down_left):
    groups, width = up_right.shape[0], up_right.shape[2]
    mp_ways, dp_ways = lax.axis_size("mp"), lax.axis_size("dp")
    scale = (dp_ways * tokens.shape[0]) ** (-0.5)
    me = jnp.stack([lax.axis_index("mp"), lax.axis_index("dp")]).astype(jnp.int32)
    firsts, seconds, mid_sums, last_sums = [], [], [], []
    for q in range(groups):
        firsts.append(exchange(make_panels(me, tokens, cotangent, up_right, down_left, q, mp_ways)))
    for q in range(groups):
        panels, halves = make_middle(me, firsts[q], up_left, down_first_factor, q, dp_ways)
        seconds.append(exchange(panels))
        mid_sums.append(halving_sums(halves, scale))
    for q in range(groups):
        halves = make_last_grads(me, seconds[q], tokens, cotangent, width, dp_ways)
        last_sums.append(halving_sums(halves, scale))
    mixed, tokens_grad = make_outputs(me, seconds, down_left, up_right)

    def pick(sums, kind):
        return jnp.stack([s[kind] for s in sums])

    return (mixed, tokens_grad, pick(last_sums, 1), pick(mid_sums, 1), pick(mid_sums, 0), pick(last_sums, 0))


def solution(mesh):
    weight = P(None, "mp", None, None)
    in_specs = (P("dp", "mp"), P("dp", "mp"), weight, weight, weight, weight)
    grad = P(None, "mp", "dp", None)
    out_specs = (P("dp", "mp"), P("dp", "mp"), grad, grad, grad, grad)
    return jax.shard_map(body, mesh=mesh, in_specs=in_specs, out_specs=out_specs, check_vma=False)
```

```python
import functools

import jax
import jax.numpy as jnp
from jax import lax
from jax.experimental import pallas as pl
from jax.experimental.pallas import tpu as pltpu
from jax.sharding import PartitionSpec as P

gelu_root = 0.7978845608
gelu_cube = 0.044715
F32 = jnp.float32
BF16 = jnp.bfloat16


def mm(lhs, rhs, ldim, rdim):
    return lax.dot_general(lhs, rhs, (((ldim,), (rdim,)), ((), ())), preferred_element_type=F32)


def send_panel(outs, kind, scratch, me, blocks):
    span = blocks * blocks
    for k, out in enumerate(outs):
        start = pl.multiple_of((me ^ k) * span, span)
        rows = scratch[pl.ds(start, span), :]
        out[kind] = rows.reshape(out.shape[1:]).astype(BF16)


def gather_rows(parts, kind, scratch, slot, me, block, blocks):
    for k, part in enumerate(parts):
        start = pl.multiple_of((me ^ k) * blocks, blocks)
        scratch[slot, pl.ds(start, blocks), :] = part[kind, block].astype(F32)
    return scratch[slot].astype(BF16)


def hop_order(ways, kind):
    bits = [1 << b for b in range(ways.bit_length() - 1)]
    return [bits[1], bits[0]] + bits[2:] if kind and len(bits) > 1 else bits


def store_grad(outs, kind, block, value, scratch, slot, me, ways):
    rows = value.shape[0] // ways
    first, *later = hop_order(ways, kind)
    scratch[slot] = value
    for p in range(ways // 2):
        rel = sum(bit for t, bit in enumerate(later) if p >> t & 1)
        for out, target in ((outs[2 * kind], rel), (outs[2 * kind + 1], rel + first)):
            start = pl.multiple_of((me ^ target) * rows, rows)
            out[p, block] = scratch[slot, pl.ds(start, rows), :].astype(BF16)


def panels_kernel(ways, me_ref, x_ref, g_ref, ur_ref, dl_ref, *rest):
    outs, scr_r, scr_b = rest[:ways], rest[ways], rest[ways + 1]
    blocks, width = ur_ref.shape[1], ur_ref.shape[2]
    me = me_ref[0]
    for i in range(blocks):
        cols = slice(i * width, (i + 1) * width)
        scr_r[pl.ds(i, width, stride=blocks), :] = mm(ur_ref[0, i], x_ref[:, cols], 0, 1)
        scr_b[pl.ds(i, width, stride=blocks), :] = mm(dl_ref[0, i], g_ref[:, cols], 1, 1)
    send_panel(outs, 0, scr_r, me, blocks)
    send_panel(outs, 1, scr_b, me, blocks)


def full_spec(shape):
    return pl.BlockSpec(shape, lambda s: (0,) * len(shape))


def group_spec(w, q):
    return pl.BlockSpec((1,) + w.shape[1:], lambda s: (q, 0, 0, 0))


def limits(flops, mib):
    return dict(
        compiler_params=pltpu.CompilerParams(vmem_limit_bytes=40 * 2**20),
        cost_estimate=pl.CostEstimate(flops=flops * 8, bytes_accessed=mib * 2**20, transcendentals=0),
    )


def make_panels(me, x, g, ur, dl, q, ways):
    tok, blocks, width = x.shape[0], ur.shape[1], ur.shape[2]
    part = jax.ShapeDtypeStruct((2, blocks, blocks, tok), BF16)
    return pl.pallas_call(
        functools.partial(panels_kernel, ways),
        out_shape=[part] * ways,
        grid=(1,),
        in_specs=[
            pl.BlockSpec(memory_space=pltpu.SMEM),
            full_spec(x.shape),
            full_spec(g.shape),
            group_spec(ur, q),
            group_spec(dl, q),
        ],
        out_specs=[full_spec(part.shape)] * ways,
        scratch_shapes=[pltpu.VMEM((width * blocks, tok), F32)] * 2,
        **limits(4 * tok * blocks * width * width, 8),
    )(me, x, g, ur, dl)


UNROLL = 4


def middle_kernel(mp_ways, dp_ways, me_ref, ul_ref, df_ref, *rest):
    n = mp_ways
    first_in, outs, grads = rest[:n], rest[n : 2 * n], rest[2 * n : 2 * n + 4]
    scr_d, scr_u, asm_r, asm_b, gr1, gr2 = rest[2 * n + 4 :]
    blocks, width = ul_ref.shape[1], ul_ref.shape[2]
    me_mp, me_dp = me_ref[0], me_ref[1]

    def one(c, slot):
        ul, df = ul_ref[0, c], df_ref[0, c]
        cu = gather_rows(first_in, 0, asm_r, slot, me_mp, c, blocks)
        dg = gather_rows(first_in, 1, asm_b, slot, me_mp, c, blocks)
        pre = mm(ul, cu, 0, 0)
        sq = pre * pre
        th = jnp.tanh(gelu_root * (pre + gelu_cube * sq * pre))
        half = 0.5 * (1.0 + th)
        hidden = (pre * half).astype(BF16)
        slope = half + 0.5 * pre * (1.0 - th * th) * (gelu_root * (1.0 + 3.0 * gelu_cube * sq))
        scr_d[pl.ds(c, width, stride=blocks), :] = mm(df, hidden, 0, 0)
        pg = (mm(df, dg, 1, 0) * slope).astype(BF16)
        scr_u[pl.ds(c, width, stride=blocks), :] = mm(ul, pg, 1, 0)
        store_grad(grads, 0, c, mm(hidden, dg, 1, 1), gr1, slot, me_dp, dp_ways)
        store_grad(grads, 1, c, mm(cu, pg, 1, 1), gr2, slot, me_dp, dp_ways)

    def step(s, carry):
        for slot in range(UNROLL):
            one(s * UNROLL + slot, slot)
        return carry

    lax.fori_loop(0, blocks // UNROLL, step, 0)
    send_panel(outs, 0, scr_d, me_mp, blocks)
    send_panel(outs, 1, scr_u, me_mp, blocks)


def grad_halves(blocks, width, dp_ways):
    return jax.ShapeDtypeStruct((dp_ways // 2, blocks, width // dp_ways, width), BF16)


def make_middle(me, first_in, ul, df, q, dp_ways):
    n = len(first_in)
    part = jax.ShapeDtypeStruct(first_in[0].shape, BF16)
    blocks, width, tok = ul.shape[1], ul.shape[2], part.shape[3]
    half = grad_halves(blocks, width, dp_ways)
    res = pl.pallas_call(
        functools.partial(middle_kernel, n, dp_ways),
        out_shape=[part] * n + [half] * 4,
        grid=(1,),
        in_specs=[pl.BlockSpec(memory_space=pltpu.SMEM)] + [group_spec(ul, q)] * 2 + [full_spec(part.shape)] * n,
        out_specs=[full_spec(part.shape)] * n + [full_spec(half.shape)] * 4,
        scratch_shapes=[pltpu.VMEM((width * blocks, tok), F32)] * 2
        + [pltpu.VMEM((UNROLL, width, tok), F32)] * 2
        + [pltpu.VMEM((UNROLL, width, width), F32)] * 2,
        **limits(12 * tok * blocks * width * width, 8),
    )(me, ul, df, *first_in)
    return res[:n], res[n:]


def last_grads_kernel(mp_ways, dp_ways, me_ref, x_ref, g_ref, *rest):
    n = mp_ways
    second_in, grads = rest[:n], rest[n : n + 4]
    asm_d, asm_u, gr1, gr2 = rest[n + 4 :]
    blocks = second_in[0].shape[1]
    width = gr1.shape[1]
    me_mp, me_dp = me_ref[0], me_ref[1]
    for e in range(blocks):
        cols = slice(e * width, (e + 1) * width)
        slot = e % UNROLL
        cd = gather_rows(second_in, 0, asm_d, slot, me_mp, e, blocks)
        rg = gather_rows(second_in, 1, asm_u, slot, me_mp, e, blocks)
        store_grad(grads, 0, e, mm(cd, g_ref[:, cols], 1, 0), gr1, slot, me_dp, dp_ways)
        store_grad(grads, 1, e, mm(rg, x_ref[:, cols], 1, 0).T, gr2, slot, me_dp, dp_ways)


def make_last_grads(me, second_in, x, g, width, dp_ways):
    n = len(second_in)
    part = second_in[0]
    blocks, tok = part.shape[1], part.shape[3]
    half = grad_halves(blocks, width, dp_ways)
    return pl.pallas_call(
        functools.partial(last_grads_kernel, n, dp_ways),
        out_shape=[half] * 4,
        grid=(1,),
        in_specs=[pl.BlockSpec(memory_space=pltpu.SMEM)] + [full_spec(x.shape)] * 2 + [full_spec(part.shape)] * n,
        out_specs=[full_spec(half.shape)] * 4,
        scratch_shapes=[pltpu.VMEM((UNROLL, width, tok), F32)] * 2 + [pltpu.VMEM((UNROLL, width, width), F32)] * 2,
        **limits(4 * tok * blocks * width * width, 6),
    )(me, x, g, *second_in)


def outputs_kernel(mp_ways, me_ref, dl_ref, ur_ref, *rest):
    n = mp_ways
    groups = dl_ref.shape[0]
    second_in = rest[: groups * n]
    mixed, tgrad, asm_d, asm_u = rest[groups * n :]
    blocks, width = dl_ref.shape[1], dl_ref.shape[2]
    me_mp = me_ref[0]
    for e in range(blocks):
        cols = slice(e * width, (e + 1) * width)
        out_sum = grad_sum = None
        for q in range(groups):
            parts = second_in[q * n : (q + 1) * n]
            slot = (e * groups + q) % UNROLL
            cd = gather_rows(parts, 0, asm_d, slot, me_mp, e, blocks)
            rg = gather_rows(parts, 1, asm_u, slot, me_mp, e, blocks)
            one = mm(cd, dl_ref[q, e], 0, 0)
            two = mm(ur_ref[q, e], rg, 1, 0)
            out_sum = one if q == 0 else out_sum + one
            grad_sum = two if q == 0 else grad_sum + two
        mixed[:, cols] = out_sum.astype(BF16)
        tgrad[:, cols] = grad_sum.T.astype(BF16)


def make_outputs(me, second_in, dl, ur):
    n = len(second_in[0])
    part = second_in[0][0]
    groups, blocks, width, tok = dl.shape[0], dl.shape[1], dl.shape[2], part.shape[3]
    out = jax.ShapeDtypeStruct((tok, blocks * width), BF16)
    return pl.pallas_call(
        functools.partial(outputs_kernel, n),
        out_shape=[out] * 2,
        grid=(1,),
        in_specs=[pl.BlockSpec(memory_space=pltpu.SMEM)]
        + [full_spec(dl.shape)] * 2
        + [full_spec(part.shape)] * (n * groups),
        out_specs=[full_spec(out.shape)] * 2,
        scratch_shapes=[pltpu.VMEM((UNROLL, width, tok), F32)] * 2,
        **limits(8 * tok * blocks * width * width, 10),
    )(me, dl, ur, *[p for parts in second_in for p in parts])


def xor_permute(array, axis, k):
    return lax.ppermute(array, axis, [(i, i ^ k) for i in range(lax.axis_size(axis))])


def exchange(parts):
    return [p if k == 0 else xor_permute(p, "mp", k) for k, p in enumerate(parts)]


def halving_rounds(reductions, scale):
    ways = lax.axis_size("dp")
    orders = [hop_order(ways, kind) for kind in range(2)]
    hops = len(orders[0])
    pairs = [[[h[0], h[1]], [h[2], h[3]]] for h in reductions]
    sums = [[None, None] for _ in reductions]
    for turn in range(hops + len(reductions) - 1):
        active = [(s, kind) for s in range(len(reductions)) if 0 <= turn - s < hops for kind in range(2)]
        got = [xor_permute(pairs[s][kind][1], "dp", orders[kind][turn - s]) for s, kind in active]
        got = lax.optimization_barrier(got)
        for (s, kind), arrived in zip(active, got):
            total = pairs[s][kind][0].astype(F32) + arrived.astype(F32)
            if total.shape[0] == 1:
                sums[s][kind] = total[0] * scale
                continue
            total = total.astype(BF16).reshape((total.shape[0] // 2, 2) + total.shape[1:])
            pairs[s][kind] = [total[:, 0], total[:, 1]]
    return sums


def body(tokens, cotangent, up_right, up_left, down_first_factor, down_left):
    groups, width = up_right.shape[0], up_right.shape[2]
    mp_ways, dp_ways = lax.axis_size("mp"), lax.axis_size("dp")
    scale = (dp_ways * tokens.shape[0]) ** (-0.5)
    me = jnp.stack([lax.axis_index("mp"), lax.axis_index("dp")]).astype(jnp.int32)
    firsts, seconds, reductions = [], [], []
    for q in range(groups):
        firsts.append(exchange(make_panels(me, tokens, cotangent, up_right, down_left, q, mp_ways)))
    for q in range(groups):
        panels, halves = make_middle(me, firsts[q], up_left, down_first_factor, q, dp_ways)
        seconds.append(exchange(panels))
        reductions.append(halves)
    for q in range(groups):
        reductions.append(make_last_grads(me, seconds[q], tokens, cotangent, width, dp_ways))
    sums = halving_rounds(reductions, scale)
    mid_sums, last_sums = sums[:groups], sums[groups:]
    mixed, tokens_grad = make_outputs(me, seconds, down_left, up_right)

    def pick(sums, kind):
        return jnp.stack([s[kind] for s in sums])

    return (mixed, tokens_grad, pick(last_sums, 1), pick(mid_sums, 1), pick(mid_sums, 0), pick(last_sums, 0))


def solution(mesh):
    weight = P(None, "mp", None, None)
    in_specs = (P("dp", "mp"), P("dp", "mp"), weight, weight, weight, weight)
    grad = P(None, "mp", "dp", None)
    out_specs = (P("dp", "mp"), P("dp", "mp"), grad, grad, grad, grad)
    return jax.shard_map(body, mesh=mesh, in_specs=in_specs, out_specs=out_specs, check_vma=False)
```

```python
import functools

import jax
import jax.numpy as jnp
from jax import lax
from jax.experimental import pallas as pl
from jax.experimental.pallas import tpu as pltpu
from jax.sharding import PartitionSpec as P

gelu_root = 0.7978845608
gelu_cube = 0.044715
F32 = jnp.float32
BF16 = jnp.bfloat16


def mm(lhs, rhs, ldim, rdim):
    return lax.dot_general(lhs, rhs, (((ldim,), (rdim,)), ((), ())), preferred_element_type=F32)


def send_panel(outs, kind, scratch, me, blocks):
    span = blocks * blocks
    for k, out in enumerate(outs):
        start = pl.multiple_of((me ^ k) * span, span)
        rows = scratch[pl.ds(start, span), :]
        out[kind] = rows.reshape(out.shape[1:]).astype(BF16)


def gather_rows(parts, kind, scratch, slot, me, block, blocks):
    for k, part in enumerate(parts):
        start = pl.multiple_of((me ^ k) * blocks, blocks)
        scratch[slot, pl.ds(start, blocks), :] = part[kind, block].astype(F32)
    return scratch[slot].astype(BF16)


def hop_order(ways, kind):
    bits = [1 << b for b in range(ways.bit_length() - 1)]
    return [bits[1], bits[0]] + bits[2:] if kind and len(bits) > 1 else bits


def store_grad(outs, kind, block, value, scratch, slot, me, ways):
    rows = value.shape[0] // ways
    first, *later = hop_order(ways, kind)
    scratch[slot] = value
    for p in range(ways // 2):
        rel = sum(bit for t, bit in enumerate(later) if p >> t & 1)
        for out, target in ((outs[2 * kind], rel), (outs[2 * kind + 1], rel + first)):
            start = pl.multiple_of((me ^ target) * rows, rows)
            out[p, block] = scratch[slot, pl.ds(start, rows), :].astype(BF16)


def panels_kernel(ways, me_ref, x_ref, g_ref, ur_ref, dl_ref, *rest):
    outs, scr_r, scr_b = rest[:ways], rest[ways], rest[ways + 1]
    blocks, width = ur_ref.shape[1], ur_ref.shape[2]
    me = me_ref[0]
    for i in range(blocks):
        cols = slice(i * width, (i + 1) * width)
        scr_r[pl.ds(i, width, stride=blocks), :] = mm(ur_ref[0, i], x_ref[:, cols], 0, 1)
        scr_b[pl.ds(i, width, stride=blocks), :] = mm(dl_ref[0, i], g_ref[:, cols], 1, 1)
    send_panel(outs, 0, scr_r, me, blocks)
    send_panel(outs, 1, scr_b, me, blocks)


def full_spec(shape):
    return pl.BlockSpec(shape, lambda s: (0,) * len(shape))


def group_spec(w, q):
    return pl.BlockSpec((1,) + w.shape[1:], lambda s: (q, 0, 0, 0))


def limits(flops, mib):
    return dict(
        compiler_params=pltpu.CompilerParams(vmem_limit_bytes=40 * 2**20),
        cost_estimate=pl.CostEstimate(flops=flops * 8, bytes_accessed=mib * 2**20, transcendentals=0),
    )


def make_panels(me, x, g, ur, dl, q, ways):
    tok, blocks, width = x.shape[0], ur.shape[1], ur.shape[2]
    part = jax.ShapeDtypeStruct((2, blocks, blocks, tok), BF16)
    return pl.pallas_call(
        functools.partial(panels_kernel, ways),
        out_shape=[part] * ways,
        grid=(1,),
        in_specs=[
            pl.BlockSpec(memory_space=pltpu.SMEM),
            full_spec(x.shape),
            full_spec(g.shape),
            group_spec(ur, q),
            group_spec(dl, q),
        ],
        out_specs=[full_spec(part.shape)] * ways,
        scratch_shapes=[pltpu.VMEM((width * blocks, tok), F32)] * 2,
        **limits(4 * tok * blocks * width * width, 8),
    )(me, x, g, ur, dl)


UNROLL = 4


def middle_kernel(mp_ways, dp_ways, me_ref, ul_ref, df_ref, *rest):
    n = mp_ways
    first_in, outs, grads = rest[:n], rest[n : 2 * n], rest[2 * n : 2 * n + 4]
    scr_d, scr_u, asm_r, asm_b, gr1, gr2 = rest[2 * n + 4 :]
    blocks, width = ul_ref.shape[1], ul_ref.shape[2]
    me_mp, me_dp = me_ref[0], me_ref[1]

    def one(c, slot):
        ul, df = ul_ref[0, c], df_ref[0, c]
        cu = gather_rows(first_in, 0, asm_r, slot, me_mp, c, blocks)
        dg = gather_rows(first_in, 1, asm_b, slot, me_mp, c, blocks)
        pre = mm(ul, cu, 0, 0)
        sq = pre * pre
        th = jnp.tanh(gelu_root * (pre + gelu_cube * sq * pre))
        half = 0.5 * (1.0 + th)
        hidden = (pre * half).astype(BF16)
        slope = half + 0.5 * pre * (1.0 - th * th) * (gelu_root * (1.0 + 3.0 * gelu_cube * sq))
        scr_d[pl.ds(c, width, stride=blocks), :] = mm(df, hidden, 0, 0)
        pg = (mm(df, dg, 1, 0) * slope).astype(BF16)
        scr_u[pl.ds(c, width, stride=blocks), :] = mm(ul, pg, 1, 0)
        store_grad(grads, 0, c, mm(hidden, dg, 1, 1), gr1, slot, me_dp, dp_ways)
        store_grad(grads, 1, c, mm(cu, pg, 1, 1), gr2, slot, me_dp, dp_ways)

    def step(s, carry):
        for slot in range(UNROLL):
            one(s * UNROLL + slot, slot)
        return carry

    lax.fori_loop(0, blocks // UNROLL, step, 0)
    send_panel(outs, 0, scr_d, me_mp, blocks)
    send_panel(outs, 1, scr_u, me_mp, blocks)


def grad_halves(blocks, width, dp_ways):
    return jax.ShapeDtypeStruct((dp_ways // 2, blocks, width // dp_ways, width), BF16)


def make_middle(me, first_in, ul, df, q, dp_ways):
    n = len(first_in)
    part = jax.ShapeDtypeStruct(first_in[0].shape, BF16)
    blocks, width, tok = ul.shape[1], ul.shape[2], part.shape[3]
    half = grad_halves(blocks, width, dp_ways)
    res = pl.pallas_call(
        functools.partial(middle_kernel, n, dp_ways),
        out_shape=[part] * n + [half] * 4,
        grid=(1,),
        in_specs=[pl.BlockSpec(memory_space=pltpu.SMEM)] + [group_spec(ul, q)] * 2 + [full_spec(part.shape)] * n,
        out_specs=[full_spec(part.shape)] * n + [full_spec(half.shape)] * 4,
        scratch_shapes=[pltpu.VMEM((width * blocks, tok), F32)] * 2
        + [pltpu.VMEM((UNROLL, width, tok), F32)] * 2
        + [pltpu.VMEM((UNROLL, width, width), F32)] * 2,
        **limits(12 * tok * blocks * width * width, 8),
    )(me, ul, df, *first_in)
    return res[:n], res[n:]


def last_grads_kernel(groups, dp_ways, me_ref, x_ref, g_ref, *rest):
    count = len(rest) - 8
    n = count // groups
    second_in, grads = rest[:count], rest[count : count + 4]
    asm_d, asm_u, gr1, gr2 = rest[count + 4 :]
    blocks = second_in[0].shape[1]
    width = gr1.shape[1]
    me_mp, me_dp = me_ref[0], me_ref[1]
    for q in range(groups):
        parts = second_in[q * n : (q + 1) * n]
        for e in range(blocks):
            cols = slice(e * width, (e + 1) * width)
            slot = e % UNROLL
            cd = gather_rows(parts, 0, asm_d, slot, me_mp, e, blocks)
            rg = gather_rows(parts, 1, asm_u, slot, me_mp, e, blocks)
            down = mm(cd, g_ref[:, cols], 1, 0)
            right = mm(rg, x_ref[:, cols], 1, 0).T
            store_grad(grads, 0, q * blocks + e, down, gr1, slot, me_dp, dp_ways)
            store_grad(grads, 1, q * blocks + e, right, gr2, slot, me_dp, dp_ways)


def make_last_grads(me, seconds, x, g, width, dp_ways):
    groups = len(seconds)
    parts = [p for second in seconds for p in second]
    part = parts[0]
    blocks, tok = part.shape[1], part.shape[3]
    half = grad_halves(groups * blocks, width, dp_ways)
    return pl.pallas_call(
        functools.partial(last_grads_kernel, groups, dp_ways),
        out_shape=[half] * 4,
        grid=(1,),
        in_specs=[pl.BlockSpec(memory_space=pltpu.SMEM)] + [full_spec(x.shape)] * 2 + [full_spec(part.shape)] * len(parts),
        out_specs=[full_spec(half.shape)] * 4,
        scratch_shapes=[pltpu.VMEM((UNROLL, width, tok), F32)] * 2 + [pltpu.VMEM((UNROLL, width, width), F32)] * 2,
        **limits(4 * groups * tok * blocks * width * width, 12),
    )(me, x, g, *parts)


def outputs_kernel(mp_ways, me_ref, dl_ref, ur_ref, *rest):
    n = mp_ways
    groups = dl_ref.shape[0]
    second_in = rest[: groups * n]
    mixed, tgrad, asm_d, asm_u = rest[groups * n :]
    blocks, width = dl_ref.shape[1], dl_ref.shape[2]
    me_mp = me_ref[0]
    for e in range(blocks):
        cols = slice(e * width, (e + 1) * width)
        out_sum = grad_sum = None
        for q in range(groups):
            parts = second_in[q * n : (q + 1) * n]
            slot = (e * groups + q) % UNROLL
            cd = gather_rows(parts, 0, asm_d, slot, me_mp, e, blocks)
            rg = gather_rows(parts, 1, asm_u, slot, me_mp, e, blocks)
            one = mm(cd, dl_ref[q, e], 0, 0)
            two = mm(ur_ref[q, e], rg, 1, 0)
            out_sum = one if q == 0 else out_sum + one
            grad_sum = two if q == 0 else grad_sum + two
        mixed[:, cols] = out_sum.astype(BF16)
        tgrad[:, cols] = grad_sum.T.astype(BF16)


def make_outputs(me, second_in, dl, ur):
    n = len(second_in[0])
    part = second_in[0][0]
    groups, blocks, width, tok = dl.shape[0], dl.shape[1], dl.shape[2], part.shape[3]
    out = jax.ShapeDtypeStruct((tok, blocks * width), BF16)
    return pl.pallas_call(
        functools.partial(outputs_kernel, n),
        out_shape=[out] * 2,
        grid=(1,),
        in_specs=[pl.BlockSpec(memory_space=pltpu.SMEM)]
        + [full_spec(dl.shape)] * 2
        + [full_spec(part.shape)] * (n * groups),
        out_specs=[full_spec(out.shape)] * 2,
        scratch_shapes=[pltpu.VMEM((UNROLL, width, tok), F32)] * 2,
        **limits(8 * tok * blocks * width * width, 10),
    )(me, dl, ur, *[p for parts in second_in for p in parts])


def xor_permute(array, axis, k):
    return lax.ppermute(array, axis, [(i, i ^ k) for i in range(lax.axis_size(axis))])


def exchange(parts):
    return [p if k == 0 else xor_permute(p, "mp", k) for k, p in enumerate(parts)]


def halving_rounds(reductions, scale):
    ways = lax.axis_size("dp")
    orders = [hop_order(ways, kind) for kind in range(2)]
    hops = len(orders[0])
    pairs = [[[h[0], h[1]], [h[2], h[3]]] for h in reductions]
    sums = [[None, None] for _ in reductions]
    for turn in range(hops + len(reductions) - 1):
        active = [(s, kind) for s in range(len(reductions)) if 0 <= turn - s < hops for kind in range(2)]
        got = [xor_permute(pairs[s][kind][1], "dp", orders[kind][turn - s]) for s, kind in active]
        following = pairs[turn + 1] if turn + 1 < len(pairs) else []
        got, following = lax.optimization_barrier((got, following))
        pairs[turn + 1 : turn + 2] = [following] if following else []
        for (s, kind), arrived in zip(active, got):
            total = pairs[s][kind][0].astype(F32) + arrived.astype(F32)
            if total.shape[0] == 1:
                sums[s][kind] = total[0] * scale
                continue
            total = total.astype(BF16).reshape((total.shape[0] // 2, 2) + total.shape[1:])
            pairs[s][kind] = [total[:, 0], total[:, 1]]
    return sums


def body(tokens, cotangent, up_right, up_left, down_first_factor, down_left):
    groups, width = up_right.shape[0], up_right.shape[2]
    mp_ways, dp_ways = lax.axis_size("mp"), lax.axis_size("dp")
    scale = (dp_ways * tokens.shape[0]) ** (-0.5)
    me = jnp.stack([lax.axis_index("mp"), lax.axis_index("dp")]).astype(jnp.int32)
    firsts, seconds, reductions = [], [], []
    for q in range(groups):
        firsts.append(exchange(make_panels(me, tokens, cotangent, up_right, down_left, q, mp_ways)))
    for q in range(groups):
        panels, halves = make_middle(me, firsts[q], up_left, down_first_factor, q, dp_ways)
        seconds.append(exchange(panels))
        reductions.append(halves)
    reductions.append(make_last_grads(me, seconds, tokens, cotangent, width, dp_ways))
    sums = halving_rounds(reductions, scale)
    mid_sums, last_sums = sums[:groups], [s.reshape((groups, -1) + s.shape[1:]) for s in sums[groups]]
    mixed, tokens_grad = make_outputs(me, seconds, down_left, up_right)

    def pick(sums, kind):
        return jnp.stack([s[kind] for s in sums])

    return (mixed, tokens_grad, last_sums[1], pick(mid_sums, 1), pick(mid_sums, 0), last_sums[0])


def solution(mesh):
    weight = P(None, "mp", None, None)
    in_specs = (P("dp", "mp"), P("dp", "mp"), weight, weight, weight, weight)
    grad = P(None, "mp", "dp", None)
    out_specs = (P("dp", "mp"), P("dp", "mp"), grad, grad, grad, grad)
    return jax.shard_map(body, mesh=mesh, in_specs=in_specs, out_specs=out_specs, check_vma=False)
```
